256 devices in a mesh: orb: 8 (over y, z_hi), aux: 32 (over x, z_lo, core).
Axes of the slice: x: 4, y: 4, z: 8 (z_hi: 2, z_lo: 4; z = z_hi * 4 + z_lo), core: 2. Of those that a mesh axis runs over, the one named last changes fastest.
Arguments:
- factors: bfloat16 [16, 32768, 512], P('orb', 'aux'), may hold values from -0.5 to 0.5
- occ_energy: float32 [16], replicated, may hold values from -2 to -0.5
- virt_energy: float32 [16, 512], replicated, may hold values from 0.2 to 3
- tile_table: int32 [16, 3], replicated, may hold values from 0 to 15, as said below
Outputs:
- gamma: bfloat16 [16, 32768, 512], P('orb', 'aux')
The draws below stay inside these ranges and needn't reach their ends.
Inputs may be any that keep to these rules, and one draw needn't show every extreme that they name: Row t names two different blocks and the group tile_table[t, 2] that computes the tile. Each group computes at most 4 tiles, and some group exactly 4. Of the blocks owned by another group, the tiles of one group name at most one.
All inputs are finite; a program needn't handle non-finite values.
Results may differ from the reference program's by a relative error of at most 0.0053.
Values may be sent and summed in bfloat16 or wider, within the bound.
A program may use at most 192 MiB of HBM per device.

```python
import math
import jax
import jax.numpy as jnp
from jax import lax

VB = 512
NAUX = 32768
BLK_GRP = 2
TPG = 2
NB = 16
TILES = 16
N_ORB = 8


def draw_tile_table(key, part):
    groups = N_ORB
    owned = BLK_GRP
    keys = jax.random.split(jax.random.fold_in(key, 7), 6)
    order = jax.random.permutation(keys[0], groups)
    offsets = jax.random.randint(keys[1], (groups // 2,), 0, TPG + 1).at[0].set(TPG)
    counts = jnp.zeros((groups,), jnp.int32).at[order[0::2]].set(TPG + offsets).at[order[1::2]].set(TPG - offsets)
    limits = jnp.cumsum(counts)
    slots = jnp.arange(TILES, dtype=jnp.int32)
    sorted_helper = jnp.sum((slots[:, None] >= limits[None, :]).astype(jnp.int32), axis=1)
    helper = sorted_helper[jax.random.permutation(keys[2], TILES)]
    chosen = jax.random.randint(keys[3], (groups, groups), 0, owned)
    own_blocks = helper[:, None] * owned + jnp.arange(owned, dtype=jnp.int32)[None, :]
    other_blocks = jnp.arange(groups, dtype=jnp.int32)[None, :] * owned + chosen[helper]
    listing = jnp.concatenate([own_blocks, other_blocks], axis=1)
    count = owned + groups - 1
    first_raw = jax.random.randint(keys[4], (TILES,), 0, count)
    second_raw = (first_raw + 1 + jax.random.randint(keys[5], (TILES,), 0, count - 1)) % count
    first_pos = jnp.where(first_raw < owned + helper, first_raw, first_raw + 1)
    second_pos = jnp.where(second_raw < owned + helper, second_raw, second_raw + 1)
    first = jnp.take_along_axis(listing, first_pos[:, None], axis=1)[:, 0]
    second = jnp.take_along_axis(listing, second_pos[:, None], axis=1)[:, 0]
    return jnp.stack([first, second, helper], axis=1).astype(jnp.int32)


def block_scale(rng, extent, shards, least, top_value):
    level, own = 1.0, jax.random.fold_in(rng, 6)
    for position, shards_of in shards:
        heights = jnp.exp(jax.random.uniform(jax.random.fold_in(own, position), (shards_of,), jnp.float32, least / len(shards), top_value / len(shards)))
        level = level * jnp.repeat(heights, extent[position] // shards_of).reshape([-1 if axis == position else 1 for axis in range(len(extent))])
    return level


def noise(own_key, dims, spread, limit, cuts=(), kind=jnp.bfloat16):
    values = spread * jax.random.normal(own_key, dims, jnp.float32)
    if cuts:
        values = values * block_scale(own_key, dims, cuts, -0.22, 0.18)
    return jnp.clip(values, -limit, limit).astype(kind)


def setup_inputs(seed: int = 0) -> dict:
    key_of = jax.random.split(jax.random.key(seed), 5)
    factors = noise(key_of[0], (NB, NAUX, VB), 0.08, 0.5, ((0, 8), (1, 32)))
    occ_energy = jnp.clip(jax.random.uniform(key_of[1], (NB,), jnp.float32, -2.0, -0.5), -2.0, -0.5)
    virt_energy = jnp.clip(jnp.exp(jax.random.uniform(key_of[2], (NB, VB), jnp.float32, math.log(0.2), math.log(3.0))), 0.2, 3.0)
    tile_table = draw_tile_table(jax.random.fold_in(key_of[4], 71), 0)
    return dict(factors=factors, occ_energy=occ_energy, virt_energy=virt_energy, tile_table=tile_table)


def reference(factors, occ_energy, virt_energy, tile_table):
    def tile_amp(index):
        first = tile_table[index, 0]
        second = tile_table[index, 1]
        block_p = lax.dynamic_index_in_dim(factors, first, 0, keepdims=False)
        block_q = lax.dynamic_index_in_dim(factors, second, 0, keepdims=False)
        products = lax.dot_general(block_p, block_q, (((0,), (0,)), ((), ())), preferred_element_type=jnp.float32)
        energy_p = lax.dynamic_index_in_dim(virt_energy, first, 0, keepdims=False)
        energy_q = lax.dynamic_index_in_dim(virt_energy, second, 0, keepdims=False)
        denominators = energy_p[:, None] + energy_q[None, :] - occ_energy[first] - occ_energy[second]
        return (products / denominators).astype(jnp.bfloat16)

    amps = lax.map(tile_amp, jnp.arange(TILES, dtype=jnp.int32))

    def one_block(block):
        owner = block // BLK_GRP

        def add_tile(index, acc):
            first = tile_table[index, 0]
            second = tile_table[index, 1]
            helper = tile_table[index, 2]
            amplitudes = lax.dynamic_index_in_dim(amps, index, 0, keepdims=False)

            def contrib(unused):
                block_p = lax.dynamic_index_in_dim(factors, first, 0, keepdims=False)
                block_q = lax.dynamic_index_in_dim(factors, second, 0, keepdims=False)
                to_first = lax.dot_general(block_q, amplitudes, (((1,), (1,)), ((), ())), preferred_element_type=jnp.float32)
                to_second = jnp.dot(block_p, amplitudes, preferred_element_type=jnp.float32)
                zero = jnp.zeros(to_first.shape, jnp.float32)
                return jnp.where(first == block, to_first, zero) + jnp.where(second == block, to_second, zero)

            def nothing(unused):
                return jnp.zeros((NAUX, VB), jnp.float32)

            touches = jnp.logical_or(first == block, second == block)
            term = lax.cond(touches, contrib, nothing, 0)
            return acc.at[helper].add(term)

        acc = lax.fori_loop(0, TILES, add_tile, jnp.zeros((N_ORB, NAUX, VB), jnp.float32))
        rounded = lax.optimization_barrier(acc.astype(jnp.bfloat16)).astype(jnp.float32)
        is_owner = (jnp.arange(N_ORB, dtype=jnp.int32) == owner)[:, None, None]
        total = jnp.sum(jnp.where(is_owner, acc, rounded), axis=0)
        return total.astype(jnp.bfloat16)

    return lax.map(one_block, jnp.arange(NB, dtype=jnp.int32))
```

```python
import jax
import jax.numpy as jnp
from jax import lax
from jax.experimental import pallas as pl
from jax.experimental.pallas import tpu as pltpu
from jax.sharding import PartitionSpec as P


def products_kernel(table, factors, out):
    tile = pl.program_id(0)
    block_p = factors[table[tile, 0]]
    block_q = factors[table[tile, 1]]
    out[0] = lax.dot_general(
        block_p, block_q, (((0,), (0,)), ((), ())), preferred_element_type=jnp.float32
    )


def tile_products(tile_table, slices):
    blocks, rows, width = slices.shape
    tiles = tile_table.shape[0]
    return pl.pallas_call(
        products_kernel,
        out_shape=jax.ShapeDtypeStruct((tiles, width, width), jnp.float32),
        grid_spec=pltpu.PrefetchScalarGridSpec(
            num_scalar_prefetch=1,
            grid=(tiles,),
            in_specs=[pl.BlockSpec((blocks, rows, width), lambda t, table: (0, 0, 0))],
            out_specs=pl.BlockSpec((1, width, width), lambda t, table: (t, 0, 0)),
        ),
        name="products",
    )(tile_table, slices)


def spread_kernel(table, factors, amplitudes, out, acc):
    tile = pl.program_id(0)

    @pl.when(tile == 0)
    def _():
        acc[...] = jnp.zeros_like(acc)

    p = table[tile, 0]
    q = table[tile, 1]
    amp = amplitudes[0]
    acc[p] += lax.dot_general(
        factors[q], amp, (((1,), (1,)), ((), ())), preferred_element_type=jnp.float32
    )
    acc[q] += jnp.dot(factors[p], amp, preferred_element_type=jnp.float32)

    @pl.when(tile == pl.num_programs(0) - 1)
    def _():
        out[...] = acc[...].astype(out.dtype)


def spread(tile_table, slices, amplitudes):
    blocks, rows, width = slices.shape
    tiles = tile_table.shape[0]
    return pl.pallas_call(
        spread_kernel,
        out_shape=jax.ShapeDtypeStruct(slices.shape, slices.dtype),
        grid_spec=pltpu.PrefetchScalarGridSpec(
            num_scalar_prefetch=1,
            grid=(tiles,),
            in_specs=[
                pl.BlockSpec((blocks, rows, width), lambda t, table: (0, 0, 0)),
                pl.BlockSpec((1, width, width), lambda t, table: (t, 0, 0)),
            ],
            out_specs=pl.BlockSpec((blocks, rows, width), lambda t, table: (0, 0, 0)),
            scratch_shapes=[pltpu.VMEM((blocks, rows, width), jnp.float32)],
        ),
        name="spread",
    )(tile_table, slices, amplitudes)


def shards(factors, occ_energy, virt_energy, tile_table):
    tiles = tile_table.shape[0]
    width = factors.shape[-1]
    devices = lax.axis_size("orb") * lax.axis_size("aux")
    mine = lax.axis_index("orb") * lax.axis_size("aux") + lax.axis_index("aux")
    slices = lax.all_to_all(factors, "orb", split_axis=1, concat_axis=0, tiled=True)
    products = tile_products(tile_table, slices).reshape(tiles * width, width)
    share = lax.psum_scatter(products, ("orb", "aux"), scatter_dimension=0, tiled=True)
    rows = tiles * width // devices
    tile = mine * rows // width
    start = mine * rows % width
    p = tile_table[tile, 0]
    q = tile_table[tile, 1]
    energy_p = lax.dynamic_slice(virt_energy, (p, start), (1, rows))[0]
    energy_q = virt_energy[q]
    below = energy_p[:, None] + energy_q[None, :] - occ_energy[p] - occ_energy[q]
    amp_share = (share / below).astype(jnp.bfloat16)
    amplitudes = lax.all_gather(amp_share, ("orb", "aux"), axis=0, tiled=True)
    gamma = spread(tile_table, slices, amplitudes.reshape(tiles, width, width))
    return lax.all_to_all(gamma, "orb", split_axis=0, concat_axis=1, tiled=True)


def solution(mesh):
    return jax.shard_map(
        shards,
        mesh=mesh,
        in_specs=(P("orb", "aux", None), P(), P(), P()),
        out_specs=P("orb", "aux", None),
        check_vma=False,
    )
```

```python
import functools

import jax
import jax.numpy as jnp
from jax import lax
from jax.experimental import pallas as pl
from jax.experimental.pallas import tpu as pltpu
from jax.sharding import PartitionSpec as P

MESH = pl.DeviceIdType.MESH
STREAMS = 4
STEPS = 4
Z = 8
CORES = 2


def place():
    orb = lax.axis_index("orb")
    aux = lax.axis_index("aux")
    return dict(
        x=aux // 8, y=orb // 2, z=(orb % 2) * 4 + (aux // 2) % 4, core=aux % 2
    )


def device(x, y, z, core):
    return {"orb": y * 2 + z // 4, "aux": x * 8 + (z % 4) * 2 + core}


def partner(at, dim):
    x, y = at["x"], at["y"]
    near_x, far_x = x + 1 - 2 * (x % 2), 3 - x
    near_y, far_y = y + 1 - 2 * (y % 2), 3 - y
    if isinstance(dim, int):
        to_x = (near_x, x, far_x, x)[dim]
        to_y = (y, near_y, y, far_y)[dim]
    else:
        to_x = jnp.where(dim == 0, near_x, jnp.where(dim == 2, far_x, x))
        to_y = jnp.where(dim == 1, near_y, jnp.where(dim == 3, far_y, y))
    return device(to_x, to_y, at["z"], at["core"])


def bits_of(at):
    return (
        ((at["x"] + 1) // 2) % 2,
        ((at["y"] + 1) // 2) % 2,
        at["x"] // 2,
        at["y"] // 2,
    )


def offsets_of(bits, rows):
    table = []
    for stream in range(STREAMS):
        kept = [0]
        for step in range(STEPS):
            half = rows >> (step + 1)
            kept.append(kept[-1] + half * bits[(stream + step) % STREAMS])
        table.append(kept)
    return table


def settle_kernel(
    table, slices, below, out,
    both, send_0, send_1, send_2, send_3, recv_0, recv_1, recv_2, recv_3,
    total, z_total, z_recv, amps,
    swap_sem, rs_send, rs_recv, z_send, z_arrive, zg_send, zg_arrive,
    ag_send, ag_recv, out_send, out_recv, out_sem,
):
    at = place()
    core, z = at["core"], at["z"]
    bits = bits_of(at)
    blocks, rows, width = slices.shape
    per_core = amps.shape[0]
    stream_rows = per_core // STREAMS
    kept = offsets_of(bits, stream_rows)
    sends = (send_0, send_1, send_2, send_3)
    recvs = (recv_0, recv_1, recv_2, recv_3)
    other_core = device(at["x"], at["y"], z, 1 - core)
    last = stream_rows >> STEPS
    z_rows = last * STREAMS // Z

    def z_peer(distance):
        return (z + distance) % Z

    barrier = pltpu.get_barrier_semaphore()
    peers = [other_core]
    peers += [partner(at, dim) for dim in range(STREAMS)]
    peers += [device(at["x"], at["y"], z_peer(d), core) for d in range(1, Z)]
    for peer in peers:
        pl.semaphore_signal(barrier, inc=1, device_id=peer, device_id_type=MESH)
    pl.semaphore_wait(barrier, len(peers))

    def remote(src, dst, send_sem, recv_sem, to):
        return pltpu.make_async_remote_copy(
            src_ref=src, dst_ref=dst, send_sem=send_sem, recv_sem=recv_sem,
            device_id=to, device_id_type=MESH,
        )

    mine = both.at[:, pl.ds(pl.multiple_of(core * rows, rows), rows), :]
    theirs = both.at[:, pl.ds(pl.multiple_of((1 - core) * rows, rows), rows), :]
    swap = remote(slices, mine, swap_sem.at[0], swap_sem.at[1], other_core)
    swap.start()
    own = pltpu.make_async_copy(slices, mine, swap_sem.at[2])
    own.start()
    own.wait()
    remote(slices, theirs, swap_sem.at[0], swap_sem.at[1], other_core).wait_recv()

    tiles = per_core // width

    def product(tile):
        block_p = both[table[core * tiles + tile, 0]]
        block_q = both[table[core * tiles + tile, 1]]
        return lax.dot_general(
            block_p, block_q, (((0,), (0,)), ((), ())), preferred_element_type=jnp.float32
        )

    def bit_at(dim):
        value = bits[3]
        for index in (2, 1, 0):
            value = jnp.where(dim == index, bits[index], value)
        return value

    def first_send(stream, carry):
        send_0[stream] = product(2 * stream + 1 - bit_at(stream)).astype(send_0.dtype)
        remote(
            send_0.at[stream], recv_0.at[stream],
            rs_send.at[0, stream], rs_recv.at[0, stream], partner(at, stream),
        ).start()
        return carry

    lax.fori_loop(0, STREAMS, first_send, 0)

    def first_keep(stream, carry):
        total[stream] = product(2 * stream + bit_at(stream))
        return carry

    lax.fori_loop(0, STREAMS, first_keep, 0)

    def rs_copy(step, stream):
        return remote(
            sends[step].at[stream], recvs[step].at[stream],
            rs_send.at[step, stream], rs_recv.at[step, stream],
            partner(at, (stream + step) % STREAMS),
        )

    for step in range(1, STEPS):
        half = stream_rows >> (step + 1)
        for stream in range(STREAMS):
            bit = bits[(stream + step) % STREAMS]
            rs_copy(step - 1, stream).wait_recv()
            base = kept[stream][step] - kept[stream][1]
            away = pl.multiple_of(base + half * (1 - bit), half)
            sends[step][stream] = (
                total[stream, pl.ds(away, half), :]
                + recvs[step - 1][stream, pl.ds(pl.multiple_of(half * (1 - bit), half), half), :]
            ).astype(send_0.dtype)
            rs_copy(step, stream).start()
        for stream in range(STREAMS):
            bit = bits[(stream + step) % STREAMS]
            base = kept[stream][step] - kept[stream][1]
            stay = pl.multiple_of(base + half * bit, half)
            total[stream, pl.ds(stay, half), :] += recvs[step - 1][
                stream, pl.ds(pl.multiple_of(half * bit, half), half), :
            ].astype(jnp.float32)

    for stream in range(STREAMS):
        rs_copy(STEPS - 1, stream).wait_recv()
        base = pl.multiple_of(kept[stream][STEPS] - kept[stream][1], last)
        z_total[pl.ds(stream * last, last), :] = (
            total[stream, pl.ds(base, last), :] + recvs[STEPS - 1][stream].astype(jnp.float32)
        )

    def z_copy(distance):
        to = z_peer(distance)
        return remote(
            z_total.at[pl.ds(pl.multiple_of(to * z_rows, z_rows), z_rows), :],
            z_recv.at[distance - 1],
            z_send.at[distance - 1], z_arrive.at[distance - 1],
            device(at["x"], at["y"], to, core),
        )

    for distance in range(1, Z):
        z_copy(distance).start()
    share = z_total[pl.ds(pl.multiple_of(z * z_rows, z_rows), z_rows), :]
    for distance in range(1, Z):
        z_copy(distance).wait_recv()
        share = share + z_recv[distance - 1]

    def settled(height):
        stream = height // (Z // STREAMS)
        start = kept[0][STEPS]
        for index in range(1, STREAMS):
            start = jnp.where(
                stream == index, index * stream_rows + kept[index][STEPS], start
            )
        return amps.at[
            pl.ds(pl.multiple_of(start + (height % (Z // STREAMS)) * z_rows, z_rows), z_rows), :
        ]

    settled(z)[...] = (share / below[...]).astype(amps.dtype)

    def zg_copy(distance, source, to):
        return remote(
            settled(source), settled(source),
            zg_send.at[distance - 1], zg_arrive.at[distance - 1],
            device(at["x"], at["y"], to, core),
        )

    for distance in range(1, Z):
        zg_copy(distance, z, z_peer(distance)).start()
    for distance in range(1, Z):
        zg_copy(distance, z_peer(Z - distance), z_peer(Z - distance)).wait_recv()

    def ag_rows(step, stream, arriving):
        size = stream_rows >> (step + 1)
        bit = bits[(stream + step) % STREAMS]
        if arriving:
            bit = 1 - bit
        start = stream * stream_rows + kept[stream][step] + size * bit
        return pl.ds(pl.multiple_of(start, size), size)

    def ag_copy(step, stream, arriving):
        piece = amps.at[ag_rows(step, stream, arriving), :]
        return remote(
            piece, piece, ag_send.at[step, stream], ag_recv.at[step, stream],
            partner(at, (stream + step) % STREAMS),
        )

    def out_copies(index, stream, arriving):
        slot = index * STREAMS + stream
        rows_here = ag_rows(0, stream, arriving)
        start = ag_rows(0, stream, arriving).start
        size = stream_rows // 2
        piece = amps.at[rows_here, :]
        here = out.at[pl.ds(pl.multiple_of(core * per_core + start, size), size), :]
        there = out.at[pl.ds(pl.multiple_of((1 - core) * per_core + start, size), size), :]
        across = remote(piece, here, out_send.at[slot], out_recv.at[slot], other_core)
        from_other = remote(piece, there, out_send.at[slot], out_recv.at[slot], other_core)
        return across, pltpu.make_async_copy(piece, here, out_sem.at[slot]), from_other

    for step in range(STEPS - 1, -1, -1):
        for stream in range(STREAMS):
            if step < STEPS - 1:
                ag_copy(step + 1, stream, True).wait_recv()
            ag_copy(step, stream, False).start()
    for stream in range(STREAMS):
        across, local, _ = out_copies(0, stream, False)
        across.start()
        local.start()
    for stream in range(STREAMS):
        ag_copy(0, stream, True).wait_recv()
        across, local, _ = out_copies(1, stream, True)
        across.start()
        local.start()

    swap.wait_send()
    for step in range(STEPS):
        for stream in range(STREAMS):
            rs_copy(step, stream).wait_send()
            ag_copy(step, stream, False).wait_send()
    for distance in range(1, Z):
        z_copy(distance).wait_send()
        zg_copy(distance, z, z_peer(distance)).wait_send()
    for index in range(2):
        for stream in range(STREAMS):
            across, local, from_other = out_copies(index, stream, index == 1)
            across.wait_send()
            from_other.wait_recv()
            local.wait()


def settle(tile_table, slices, below):
    blocks, rows, width = slices.shape
    tiles = tile_table.shape[0]
    per_core = tiles * width // CORES
    stream_rows = per_core // STREAMS
    halves = [stream_rows >> (step + 1) for step in range(STEPS)]
    wire = [pltpu.VMEM((STREAMS, half, width), jnp.bfloat16) for half in halves]
    last = halves[-1] * STREAMS
    dma = pltpu.SemaphoreType.DMA
    return pl.pallas_call(
        settle_kernel,
        out_shape=jax.ShapeDtypeStruct((tiles * width, width), jnp.bfloat16),
        in_specs=[
            pl.BlockSpec(memory_space=pltpu.SMEM),
            pl.BlockSpec(memory_space=pl.ANY),
            pl.BlockSpec(memory_space=pltpu.VMEM),
        ],
        out_specs=pl.BlockSpec(memory_space=pl.ANY),
        scratch_shapes=[
            pltpu.VMEM((blocks, CORES * rows, width), jnp.bfloat16),
            *wire,
            *wire,
            pltpu.VMEM((STREAMS, halves[0], width), jnp.float32),
            pltpu.VMEM((last, width), jnp.float32),
            pltpu.VMEM((Z - 1, last // Z, width), jnp.float32),
            pltpu.VMEM((per_core, width), jnp.bfloat16),
            dma((3,)),
            dma((STEPS, STREAMS)),
            dma((STEPS, STREAMS)),
            dma((Z - 1,)),
            dma((Z - 1,)),
            dma((Z - 1,)),
            dma((Z - 1,)),
            dma((STEPS, STREAMS)),
            dma((STEPS, STREAMS)),
            dma((2 * STREAMS,)),
            dma((2 * STREAMS,)),
            dma((2 * STREAMS,)),
        ],
        compiler_params=pltpu.CompilerParams(
            collective_id=0, has_side_effects=True, vmem_limit_bytes=48 << 20
        ),
        name="settle",
    )(tile_table, slices, below)


def settled_place(tiles, width):
    at = place()
    bits = bits_of(at)
    per_core = tiles * width // CORES
    stream_rows = per_core // STREAMS
    kept = offsets_of(bits, stream_rows)
    stream = at["z"] // (Z // STREAMS)
    rows = (stream_rows >> STEPS) * STREAMS // Z
    start = kept[0][STEPS]
    for index in range(1, STREAMS):
        start = jnp.where(stream == index, kept[index][STEPS], start)
    start = (
        at["core"] * per_core
        + stream * stream_rows
        + start
        + (at["z"] % (Z // STREAMS)) * rows
    )
    return start // width, start % width, rows


def spread_kernel(table, factors, amplitudes, out, acc):
    tile = pl.program_id(0)

    @pl.when(tile == 0)
    def _():
        acc[...] = jnp.zeros_like(acc)

    p = table[tile, 0]
    q = table[tile, 1]
    amp = amplitudes[0]
    acc[p] += lax.dot_general(
        factors[q], amp, (((1,), (1,)), ((), ())), preferred_element_type=jnp.float32
    )
    acc[q] += jnp.dot(factors[p], amp, preferred_element_type=jnp.float32)

    @pl.when(tile == pl.num_programs(0) - 1)
    def _():
        out[...] = acc[...].astype(out.dtype)


def spread(tile_table, slices, amplitudes):
    blocks, rows, width = slices.shape
    tiles = tile_table.shape[0]
    return pl.pallas_call(
        spread_kernel,
        out_shape=jax.ShapeDtypeStruct(slices.shape, slices.dtype),
        grid_spec=pltpu.PrefetchScalarGridSpec(
            num_scalar_prefetch=1,
            grid=(tiles,),
            in_specs=[
                pl.BlockSpec((blocks, rows, width), lambda t, table: (0, 0, 0)),
                pl.BlockSpec((1, width, width), lambda t, table: (t, 0, 0)),
            ],
            out_specs=pl.BlockSpec((blocks, rows, width), lambda t, table: (0, 0, 0)),
            scratch_shapes=[pltpu.VMEM((blocks, rows, width), jnp.float32)],
        ),
        name="spread",
    )(tile_table, slices, amplitudes)


def shards(factors, occ_energy, virt_energy, tile_table):
    tiles = tile_table.shape[0]
    width = factors.shape[-1]
    slices = lax.all_to_all(factors, "orb", split_axis=1, concat_axis=0, tiled=True)
    tile, start, rows = settled_place(tiles, width)
    p = tile_table[tile, 0]
    q = tile_table[tile, 1]
    energy_p = lax.dynamic_slice(virt_energy, (p, start), (1, rows))[0]
    energy_q = virt_energy[q]
    below = energy_p[:, None] + energy_q[None, :] - occ_energy[p] - occ_energy[q]
    amplitudes = settle(tile_table, slices, below)
    gamma = spread(tile_table, slices, amplitudes.reshape(tiles, width, width))
    return lax.all_to_all(gamma, "orb", split_axis=0, concat_axis=1, tiled=True)


def solution(mesh):
    return jax.shard_map(
        shards,
        mesh=mesh,
        in_specs=(P("orb", "aux", None), P(), P(), P()),
        out_specs=P("orb", "aux", None),
        check_vma=False,
    )
```

```python
import jax
import jax.numpy as jnp
from jax import lax
from jax.experimental import pallas as pl
from jax.experimental.pallas import tpu as pltpu
from jax.sharding import PartitionSpec as P

MESH = pl.DeviceIdType.MESH
STREAMS = 4
STEPS = 4
PARTS = 2
Z = 8
CORES = 2
ORB = 8
FAR_FIRST = (3, 5, 1, 7, 4, 2, 6)
NEAR_FIRST = (2, 6, 4, 1, 7, 3, 5)


def device(x, y, z, core):
    return {"orb": y * 2 + z // 4, "aux": x * 8 + (z % 4) * 2 + core}


def pick(options, index):
    if isinstance(index, int):
        return options[index]
    value = options[-1]
    for position in range(len(options) - 2, -1, -1):
        value = jnp.where(index == position, options[position], value)
    return value


def rows_at(start, size):
    return pl.ds(pl.multiple_of(start, size), size)


def kernel(
    table, occ, factors, virt, out,
    both, send_0, send_1, send_2, send_3, recv_0, recv_1, recv_2, recv_3,
    total, z_total, z_recv, amps, sums, gamma,
    in_send, in_recv, swap_send, swap_recv, rs_send, rs_recv, z_send, z_arrive,
    zg_send, zg_arrive, ag_send, ag_recv, cross_send, cross_recv, back_send, back_recv, local_sem,
):
    orb = lax.axis_index("orb")
    aux = lax.axis_index("aux")
    x, y, core = aux // 8, orb // 2, aux % 2
    z = (orb % 2) * 4 + (aux // 2) % 4
    near_x, far_x = x + 1 - 2 * (x % 2), 3 - x
    near_y, far_y = y + 1 - 2 * (y % 2), 3 - y
    bits = (((x + 1) // 2) % 2, ((y + 1) // 2) % 2, x // 2, y // 2)
    across_x = (near_x, x, far_x, x)
    across_y = (y, near_y, y, far_y)
    other_core = device(x, y, z, 1 - core)

    sends = (send_0, send_1, send_2, send_3)
    recvs = (recv_0, recv_1, recv_2, recv_3)
    owned, shard_rows, width = factors.shape
    blocks = both.shape[1]
    rows = shard_rows // ORB
    tiles = table.shape[0]
    per_core = amps.shape[1] // CORES
    core_tiles = tiles // CORES
    stream_rows = per_core // STREAMS
    last = stream_rows >> STEPS
    z_rows = last * STREAMS // Z
    columns = width // PARTS
    kept = []
    for stream in range(STREAMS):
        starts = [0]
        for step in range(STEPS):
            starts.append(
                starts[-1] + (stream_rows >> (step + 1)) * bits[(stream + step) % STREAMS]
            )
        kept.append(starts)

    def partner(dim):
        return device(pick(across_x, dim), pick(across_y, dim), z, core)

    def orb_peer(distance):
        return (orb + distance) % ORB

    def z_peer(distance):
        return (z + distance) % Z

    def z_device(height):
        return device(x, y, height, core)

    def remote(src, dst, send_sem, recv_sem, to):
        return pltpu.make_async_remote_copy(
            src_ref=src, dst_ref=dst, send_sem=send_sem, recv_sem=recv_sem,
            device_id=to, device_id_type=MESH,
        )

    barrier = pltpu.get_barrier_semaphore()
    peers = [other_core, partner(0), partner(2)]
    peers += [{"orb": orb_peer(d), "aux": aux} for d in range(1, ORB)]
    peers += [z_device(z_peer(d)) for d in range(1, Z) if d != Z // 2]
    for peer in peers:
        pl.semaphore_signal(barrier, inc=1, device_id=peer, device_id_type=MESH)
    pl.semaphore_wait(barrier, len(peers))

    def slices_of(source, which_core):
        return both.at[which_core, rows_at(source * owned, owned)]

    def in_copies(distance, source):
        to = orb_peer(distance)
        return [
            remote(
                factors.at[block, rows_at(to * rows, rows), :],
                both.at[core, source * owned + block],
                in_send.at[distance - 1, block], in_recv.at[distance - 1, block],
                {"orb": to, "aux": aux},
            )
            for block in range(owned)
        ]

    def swap_copy(distance, which_core):
        source = orb_peer(ORB - distance)
        piece = slices_of(source, which_core)
        return remote(piece, piece, swap_send.at[distance], swap_recv.at[distance], other_core)

    own_in = [
        pltpu.make_async_copy(
            factors.at[block, rows_at(orb * rows, rows), :],
            both.at[core, orb * owned + block],
            local_sem.at[0, block],
        )
        for block in range(owned)
    ]
    for distance in FAR_FIRST:
        for copy in in_copies(distance, orb):
            copy.start()
    for copy in own_in:
        copy.start()

    def tile_at(position):
        group, stream = position // STREAMS, position % STREAMS
        which_core = pick((core, 1 - core, core, 1 - core), group)
        bit = pick(bits, stream)
        bit = pick((bit, bit, 1 - bit, 1 - bit), group)
        return which_core * core_tiles + 2 * stream + bit

    dest = [table[tile_at(term // 2), term % 2] for term in range(2 * tiles)]

    def slot_of(block, before):
        slot = jnp.int32(0)
        for term in range(before):
            slot = jnp.where(dest[term] == block, term + 1, slot)
        return slot

    prev = [slot_of(dest[term], term) for term in range(2 * tiles)]
    final = [
        [slot_of(orb_peer(distance) * owned + block, 2 * tiles) for block in range(owned)]
        for distance in range(ORB)
    ]
    sums[0] = jnp.zeros(sums.shape[1:], sums.dtype)

    settle_stream = z // (Z // STREAMS)
    settle_start = settle_stream * stream_rows + (z % (Z // STREAMS)) * z_rows
    settle_start += pick([starts[STEPS] for starts in kept], settle_stream)
    settle_tile = core * core_tiles + settle_start // width
    first, second = table[settle_tile, 0], table[settle_tile, 1]
    lanes = lax.broadcasted_iota(jnp.int32, (z_rows, width), 1)
    wanted = lax.broadcasted_iota(jnp.int32, (z_rows, width), 0) + settle_start % width
    row_p = jnp.broadcast_to(virt[pl.ds(first, 1), :], (z_rows, width))
    energy_p = jnp.sum(jnp.where(lanes == wanted, row_p, 0.0), axis=1, keepdims=True)
    below = energy_p + virt[pl.ds(second, 1), :] - occ[first] - occ[second]

    for copy in own_in:
        copy.wait()
    swap_copy(0, core).start()
    for distance in NEAR_FIRST:
        for copy in in_copies(distance, orb_peer(ORB - distance)):
            copy.wait_recv()
        swap_copy(distance, core).start()
    for distance in range(ORB):
        swap_copy(distance, 1 - core).wait_recv()

    def product(tile, part):
        block_p = both[:, table[core * core_tiles + tile, 0]]
        block_q = both[
            :, table[core * core_tiles + tile, 1], :, rows_at(part * columns, columns)
        ]
        return lax.dot_general(
            block_p.reshape(CORES * rows, width),
            block_q.reshape(CORES * rows, columns),
            (((0,), (0,)), ((), ())),
            preferred_element_type=jnp.float32,
        )

    def first_send(slot, carry):
        part, stream = slot // STREAMS, slot % STREAMS
        send_0[slot] = product(2 * stream + 1 - pick(bits, stream), part).astype(send_0.dtype)
        remote(
            send_0.at[slot], recv_0.at[slot],
            rs_send.at[0, slot], rs_recv.at[0, slot], partner(stream),
        ).start()
        return carry

    lax.fori_loop(0, PARTS * STREAMS, first_send, 0)

    def first_keep(slot, carry):
        part, stream = slot // STREAMS, slot % STREAMS
        total[slot] = product(2 * stream + pick(bits, stream), part)
        return carry

    lax.fori_loop(0, PARTS * STREAMS, first_keep, 0)

    def rs_copy(step, slot):
        return remote(
            sends[step].at[slot], recvs[step].at[slot],
            rs_send.at[step, slot], rs_recv.at[step, slot],
            partner((slot % STREAMS + step) % STREAMS),
        )

    for step in range(1, STEPS):
        half = stream_rows >> (step + 1)
        for part in range(PARTS):
            slots = range(part * STREAMS, (part + 1) * STREAMS)
            for slot in slots:
                stream = slot % STREAMS
                bit = bits[(stream + step) % STREAMS]
                base = kept[stream][step] - kept[stream][1]
                rs_copy(step - 1, slot).wait_recv()
                sends[step][slot] = (
                    total[slot, rows_at(base + half * (1 - bit), half), :]
                    + recvs[step - 1][slot, rows_at(half * (1 - bit), half), :]
                ).astype(sends[step].dtype)
                rs_copy(step, slot).start()
            for slot in slots:
                stream = slot % STREAMS
                bit = bits[(stream + step) % STREAMS]
                base = kept[stream][step] - kept[stream][1]
                total[slot, rows_at(base + half * bit, half), :] += recvs[step - 1][
                    slot, rows_at(half * bit, half), :
                ].astype(jnp.float32)

    def z_copy(part, distance):
        to = z_peer(distance)
        return remote(
            z_total.at[part, rows_at(to * z_rows, z_rows), :],
            z_recv.at[part, distance - 1],
            z_send.at[part, distance - 1], z_arrive.at[part, distance - 1], z_device(to),
        )

    for part in range(PARTS):
        for stream in range(STREAMS):
            slot = part * STREAMS + stream
            rs_copy(STEPS - 1, slot).wait_recv()
            base = kept[stream][STEPS] - kept[stream][1]
            z_total[part, pl.ds(stream * last, last), :] = total[
                slot, rows_at(base, last), :
            ] + recvs[STEPS - 1][slot].astype(jnp.float32)
        for distance in range(1, Z):
            z_copy(part, distance).start()

    def settled(part, height):
        stream = height // (Z // STREAMS)
        start = core * per_core + stream * stream_rows + (height % (Z // STREAMS)) * z_rows
        start += pick([starts[STEPS] for starts in kept], stream)
        return amps.at[part, rows_at(start, z_rows), :]

    def zg_copy(part, distance, source, to):
        return remote(
            settled(part, source), settled(part, source),
            zg_send.at[part, distance - 1], zg_arrive.at[part, distance - 1], z_device(to),
        )

    for part in range(PARTS):
        share = z_total[part, rows_at(z * z_rows, z_rows), :]
        for distance in range(1, Z):
            z_copy(part, distance).wait_recv()
            share = share + z_recv[part, distance - 1]
        settled(part, z)[...] = (
            share / below[:, part * columns : (part + 1) * columns]
        ).astype(amps.dtype)
        for distance in range(1, Z):
            zg_copy(part, distance, z, z_peer(distance)).start()

    def ag_piece(step, slot, arriving):
        part, stream = slot // STREAMS, slot % STREAMS
        size = stream_rows >> (step + 1)
        bit = bits[(stream + step) % STREAMS]
        bit = 1 - bit if arriving else bit
        start = core * per_core + stream * stream_rows + kept[stream][step] + size * bit
        return amps.at[part, rows_at(start, size), :]

    def ag_copy(step, slot, arriving=False):
        piece = ag_piece(step, slot, arriving)
        return remote(
            piece, piece, ag_send.at[step, slot], ag_recv.at[step, slot],
            partner((slot % STREAMS + step) % STREAMS),
        )

    def cross_copy(late, slot, which_core):
        part, stream = slot // STREAMS, slot % STREAMS
        bit = 1 - bits[stream] if late else bits[stream]
        start = which_core * per_core + stream * stream_rows + width * bit
        piece = amps.at[part, rows_at(start, width), :]
        return remote(
            piece, piece, cross_send.at[late, slot], cross_recv.at[late, slot], other_core
        )

    for step in range(STEPS - 1, -1, -1):
        for part in range(PARTS):
            if step == STEPS - 1:
                for distance in range(1, Z):
                    source = z_peer(Z - distance)
                    zg_copy(part, distance, source, source).wait_recv()
            for stream in range(STREAMS):
                slot = part * STREAMS + stream
                if step < STEPS - 1:
                    ag_copy(step + 1, slot, True).wait_recv()
                ag_copy(step, slot).start()
                if step == 0:
                    cross_copy(0, slot, core).start()

    def terms(position):
        tile = tile_at(position)
        amp = [amps[part, rows_at(tile * width, width), :] for part in range(PARTS)]
        block_p = both[core, table[tile, 0]]
        block_q = both[core, table[tile, 1]]
        to_first = sums[prev[2 * position]]
        for part in range(PARTS):
            to_first = to_first + lax.dot_general(
                block_q[:, part * columns : (part + 1) * columns],
                amp[part],
                (((1,), (1,)), ((), ())),
                preferred_element_type=jnp.float32,
            )
        sums[2 * position + 1] = to_first
        to_second = [
            jnp.dot(block_p, amp[part], preferred_element_type=jnp.float32)
            for part in range(PARTS)
        ]
        sums[2 * position + 2] = sums[prev[2 * position + 1]] + jnp.concatenate(to_second, axis=1)

    def many_terms(group):
        for stream in range(STREAMS):
            terms(group * STREAMS + stream)

    slots = range(PARTS * STREAMS)
    many_terms(0)
    for slot in slots:
        cross_copy(0, slot, 1 - core).wait_recv()
    many_terms(1)
    for slot in slots:
        ag_copy(0, slot, True).wait_recv()
        cross_copy(1, slot, core).start()
    many_terms(2)
    for slot in slots:
        cross_copy(1, slot, 1 - core).wait_recv()
    many_terms(3)

    def back_copies(distance, source):
        to = orb_peer(distance)
        return [
            remote(
                gamma.at[distance, block], out.at[block, rows_at(source * rows, rows), :],
                back_send.at[distance - 1, block], back_recv.at[distance - 1, block],
                {"orb": to, "aux": aux},
            )
            for block in range(owned)
        ]

    def finish(distance):
        for block in range(owned):
            gamma[distance, block] = sums[final[distance][block]].astype(
                gamma.dtype
            )

    for distance in FAR_FIRST:
        finish(distance)
        for copy in back_copies(distance, orb):
            copy.start()
    finish(0)
    own_out = [
        pltpu.make_async_copy(
            gamma.at[0, block], out.at[block, rows_at(orb * rows, rows), :], local_sem.at[1, block]
        )
        for block in range(owned)
    ]
    for copy in own_out:
        copy.start()

    for distance in range(ORB):
        swap_copy(distance, core).wait_send()
    for distance in range(1, ORB):
        for copy in in_copies(distance, orb):
            copy.wait_send()
    for slot in slots:
        for step in range(STEPS):
            rs_copy(step, slot).wait_send()
            ag_copy(step, slot).wait_send()
        for late in range(2):
            cross_copy(late, slot, core).wait_send()
    for part in range(PARTS):
        for distance in range(1, Z):
            z_copy(part, distance).wait_send()
            zg_copy(part, distance, z, z_peer(distance)).wait_send()
    for distance in range(1, ORB):
        for copy in back_copies(distance, orb):
            copy.wait_send()
        for copy in back_copies(distance, orb_peer(ORB - distance)):
            copy.wait_recv()
    for copy in own_out:
        copy.wait()


def shards(factors, occ_energy, virt_energy, tile_table):
    owned, shard_rows, width = factors.shape
    blocks = owned * ORB
    rows = shard_rows // ORB
    tiles = tile_table.shape[0]
    stream_rows = tiles * width // CORES // STREAMS
    columns = width // PARTS
    slots = PARTS * STREAMS
    halves = [stream_rows >> (step + 1) for step in range(STEPS)]
    last = halves[-1] * STREAMS
    wire = [pltpu.VMEM((slots, half, columns), jnp.bfloat16) for half in halves]
    dma = pltpu.SemaphoreType.DMA
    return pl.pallas_call(
        kernel,
        out_shape=jax.ShapeDtypeStruct(factors.shape, factors.dtype),
        in_specs=[
            pl.BlockSpec(memory_space=pltpu.SMEM),
            pl.BlockSpec(memory_space=pltpu.SMEM),
            pl.BlockSpec(memory_space=pl.ANY),
            pl.BlockSpec(memory_space=pltpu.VMEM),
        ],
        out_specs=pl.BlockSpec(memory_space=pl.ANY),
        scratch_shapes=[
            pltpu.VMEM((CORES, blocks, rows, width), jnp.bfloat16),
            *wire,
            *wire,
            pltpu.VMEM((slots, halves[0], columns), jnp.float32),
            pltpu.VMEM((PARTS, last, columns), jnp.float32),
            pltpu.VMEM((PARTS, Z - 1, last // Z, columns), jnp.float32),
            pltpu.VMEM((PARTS, tiles * width, columns), jnp.bfloat16),
            pltpu.VMEM((2 * tiles + 1, rows, width), jnp.float32),
            pltpu.VMEM((ORB, owned, rows, width), jnp.bfloat16),
            dma((ORB - 1, owned)),
            dma((ORB - 1, owned)),
            dma((ORB,)),
            dma((ORB,)),
            dma((STEPS, slots)),
            dma((STEPS, slots)),
            dma((PARTS, Z - 1)),
            dma((PARTS, Z - 1)),
            dma((PARTS, Z - 1)),
            dma((PARTS, Z - 1)),
            dma((STEPS, slots)),
            dma((STEPS, slots)),
            dma((2, slots)),
            dma((2, slots)),
            dma((ORB - 1, owned)),
            dma((ORB - 1, owned)),
            dma((2, owned)),
        ],
        compiler_params=pltpu.CompilerParams(
            collective_id=0, has_side_effects=True, vmem_limit_bytes=56 << 20
        ),
        name="window",
    )(tile_table, occ_energy, factors, virt_energy)


def solution(mesh):
    return jax.shard_map(
        shards,
        mesh=mesh,
        in_specs=(P("orb", "aux", None), P(), P(), P()),
        out_specs=P("orb", "aux", None),
        check_vma=False,
    )
```

```python
import jax
import jax.numpy as jnp
from jax import lax
from jax.experimental import pallas as pl
from jax.experimental.pallas import tpu as pltpu
from jax.sharding import PartitionSpec as P

MESH = pl.DeviceIdType.MESH
STREAMS = 4
STEPS = 4
PARTS = 4
PAIR = 2
STAGE_TIME = {
    "keep": 0.5, "halve1": 5.0, "halve2": 8.0, "halve3": 10.5, "z": 12.5, "settle": 19.0,
    "gather3": 24.5, "gather2": 26.5, "gather1": 29.0, "gather0": 32.0,
}
PART_DELAY = 0.3
WIRE = (jnp.bfloat16, jnp.bfloat16, jnp.bfloat16, jnp.float32)
Z = 8
CORES = 2
ORB = 8
FAR_FIRST = (3, 5, 1, 7, 4, 2, 6)
Z_FAR_FIRST = (4, 3, 5, 2, 6, 1, 7)
NEAR_FIRST = (2, 6, 4, 1, 7, 3, 5)


def device(x, y, z, core):
    return {"orb": y * 2 + z // 4, "aux": x * 8 + (z % 4) * 2 + core}


def pick(options, index):
    if isinstance(index, int):
        return options[index]
    value = options[-1]
    for position in range(len(options) - 2, -1, -1):
        value = jnp.where(index == position, options[position], value)
    return value


def rows_at(start, size):
    return pl.ds(pl.multiple_of(start, size), size)


def kernel(
    table, occ, factors, virt, out,
    both, send_0, send_1, send_2, send_3, recv_0, recv_1, recv_2, recv_3,
    total, z_total, z_wire, z_recv, amps, sums, gamma,
    in_send, in_recv, swap_send, swap_recv, rs_send, rs_recv, z_send, z_arrive,
    zg_send, zg_arrive, ag_send, ag_recv, cross_send, cross_recv, back_send, back_recv, local_sem,
):
    orb = lax.axis_index("orb")
    aux = lax.axis_index("aux")
    x, y, core = aux // 8, orb // 2, aux % 2
    z = (orb % 2) * 4 + (aux // 2) % 4
    near_x, far_x = x + 1 - 2 * (x % 2), 3 - x
    near_y, far_y = y + 1 - 2 * (y % 2), 3 - y
    bits = (((x + 1) // 2) % 2, ((y + 1) // 2) % 2, x // 2, y // 2)
    across_x = (near_x, x, far_x, x)
    across_y = (y, near_y, y, far_y)
    other_core = device(x, y, z, 1 - core)

    sends = (send_0, send_1, send_2, send_3)
    recvs = (recv_0, recv_1, recv_2, recv_3)
    owned, shard_rows, width = factors.shape
    blocks = both.shape[1]
    rows = shard_rows // ORB
    tiles = table.shape[0]
    per_core = amps.shape[1] // CORES
    core_tiles = tiles // CORES
    stream_rows = per_core // STREAMS
    last = stream_rows >> STEPS
    z_rows = last * STREAMS // Z
    columns = width // PARTS
    kept = []
    for stream in range(STREAMS):
        starts = [0]
        for step in range(STEPS):
            starts.append(
                starts[-1] + (stream_rows >> (step + 1)) * bits[(stream + step) % STREAMS]
            )
        kept.append(starts)

    def partner(dim):
        return device(pick(across_x, dim), pick(across_y, dim), z, core)

    def orb_peer(distance):
        return (orb + distance) % ORB

    def z_peer(distance):
        return (z + distance) % Z

    def z_device(height):
        return device(x, y, height, core)

    def remote(src, dst, send_sem, recv_sem, to):
        return pltpu.make_async_remote_copy(
            src_ref=src, dst_ref=dst, send_sem=send_sem, recv_sem=recv_sem,
            device_id=to, device_id_type=MESH,
        )

    barrier = pltpu.get_barrier_semaphore()
    peers = [other_core, partner(0), partner(2)]
    peers += [{"orb": orb_peer(d), "aux": aux} for d in range(1, ORB)]
    peers += [z_device(z_peer(d)) for d in range(1, Z) if d != Z // 2]
    for peer in peers:
        pl.semaphore_signal(barrier, inc=1, device_id=peer, device_id_type=MESH)
    pl.semaphore_wait(barrier, len(peers))

    def slices_of(source, which_core):
        return both.at[which_core, rows_at(source * owned, owned)]

    def in_copies(distance, source):
        to = orb_peer(distance)
        return [
            remote(
                factors.at[block, rows_at(to * rows, rows), :],
                both.at[core, source * owned + block],
                in_send.at[distance - 1, block], in_recv.at[distance - 1, block],
                {"orb": to, "aux": aux},
            )
            for block in range(owned)
        ]

    def swap_copy(distance, which_core):
        source = orb_peer(ORB - distance)
        piece = slices_of(source, which_core)
        return remote(piece, piece, swap_send.at[distance], swap_recv.at[distance], other_core)

    own_in = [
        pltpu.make_async_copy(
            factors.at[block, rows_at(orb * rows, rows), :],
            both.at[core, orb * owned + block],
            local_sem.at[0, block],
        )
        for block in range(owned)
    ]
    for distance in FAR_FIRST:
        for copy in in_copies(distance, orb):
            copy.start()
    for copy in own_in:
        copy.start()

    def tile_at(position):
        group, stream = position // STREAMS, position % STREAMS
        which_core = pick((core, 1 - core, core, 1 - core), group)
        bit = pick(bits, stream)
        bit = pick((bit, bit, 1 - bit, 1 - bit), group)
        return which_core * core_tiles + 2 * stream + bit

    dest = [table[tile_at(term // 2), term % 2] for term in range(2 * tiles)]

    def slot_of(block, before):
        slot = jnp.int32(0)
        for term in range(before):
            slot = jnp.where(dest[term] == block, term + 1, slot)
        return slot

    prev = [slot_of(dest[term], term) for term in range(2 * tiles)]
    final = [
        [slot_of(orb_peer(distance) * owned + block, 2 * tiles) for block in range(owned)]
        for distance in range(ORB)
    ]
    sums[0] = jnp.zeros(sums.shape[1:], sums.dtype)

    settle_stream = z // (Z // STREAMS)
    settle_start = settle_stream * stream_rows + (z % (Z // STREAMS)) * z_rows
    settle_start += pick([starts[STEPS] for starts in kept], settle_stream)
    settle_tile = core * core_tiles + settle_start // width
    first, second = table[settle_tile, 0], table[settle_tile, 1]
    lanes = lax.broadcasted_iota(jnp.int32, (z_rows, width), 1)
    wanted = lax.broadcasted_iota(jnp.int32, (z_rows, width), 0) + settle_start % width
    row_p = jnp.broadcast_to(virt[pl.ds(first, 1), :], (z_rows, width))
    energy_p = jnp.sum(jnp.where(lanes == wanted, row_p, 0.0), axis=1, keepdims=True)
    below = energy_p + virt[pl.ds(second, 1), :] - occ[first] - occ[second]

    for copy in own_in:
        copy.wait()
    swap_copy(0, core).start()
    for distance in NEAR_FIRST:
        for copy in in_copies(distance, orb_peer(ORB - distance)):
            copy.wait_recv()
        swap_copy(distance, core).start()
    for distance in range(ORB):
        swap_copy(distance, 1 - core).wait_recv()

    def product(tile, pair):
        block_p = both[:, table[core * core_tiles + tile, 0]]
        block_q = both[
            :, table[core * core_tiles + tile, 1], :, pl.ds(pair * PAIR * columns, PAIR * columns)
        ]
        return lax.dot_general(
            block_p.reshape(CORES * rows, width),
            block_q.reshape(CORES * rows, PAIR * columns),
            (((0,), (0,)), ((), ())),
            preferred_element_type=jnp.float32,
        )

    def first_sends(pair):
        def body(stream, carry):
            away = product(2 * stream + 1 - pick(bits, stream), pair).astype(send_0.dtype)
            for member in range(PAIR):
                slot = (pair * PAIR + member) * STREAMS + stream
                send_0[slot] = away[:, member * columns : (member + 1) * columns]
                remote(
                    send_0.at[slot], recv_0.at[slot],
                    rs_send.at[0, slot], rs_recv.at[0, slot], partner(stream),
                ).start()
            return carry

        lax.fori_loop(0, STREAMS, body, 0)

    def first_keeps(pair):
        def body(stream, carry):
            stay = product(2 * stream + pick(bits, stream), pair)
            for member in range(PAIR):
                slot = (pair * PAIR + member) * STREAMS + stream
                total[slot] = stay[:, member * columns : (member + 1) * columns]
            return carry

        lax.fori_loop(0, STREAMS, body, 0)

    def rs_copy(step, slot):
        return remote(
            sends[step].at[slot], recvs[step].at[slot],
            rs_send.at[step, slot], rs_recv.at[step, slot],
            partner((slot % STREAMS + step) % STREAMS),
        )

    def slots_of(part):
        return range(part * STREAMS, (part + 1) * STREAMS)

    def halve(part, step):
        half = stream_rows >> (step + 1)
        for slot in slots_of(part):
            stream = slot % STREAMS
            bit = bits[(stream + step) % STREAMS]
            base = kept[stream][step] - kept[stream][1]
            rs_copy(step - 1, slot).wait_recv()
            sends[step][slot] = (
                total[slot, rows_at(base + half * (1 - bit), half), :]
                + recvs[step - 1][slot, rows_at(half * (1 - bit), half), :]
            ).astype(sends[step].dtype)
            rs_copy(step, slot).start()
        for slot in slots_of(part):
            stream = slot % STREAMS
            bit = bits[(stream + step) % STREAMS]
            base = kept[stream][step] - kept[stream][1]
            total[slot, rows_at(base + half * bit, half), :] += recvs[step - 1][
                slot, rows_at(half * bit, half), :
            ].astype(jnp.float32)

    def z_copy(part, distance):
        to = z_peer(distance)
        return remote(
            z_wire.at[part, rows_at(to * z_rows, z_rows), :],
            z_recv.at[part, distance - 1],
            z_send.at[part, distance - 1], z_arrive.at[part, distance - 1], z_device(to),
        )

    def along_z(part):
        for stream in range(STREAMS):
            slot = part * STREAMS + stream
            rs_copy(STEPS - 1, slot).wait_recv()
            base = kept[stream][STEPS] - kept[stream][1]
            summed = total[slot, rows_at(base, last), :] + recvs[STEPS - 1][slot]
            z_total[part, pl.ds(stream * last, last), :] = summed
            z_wire[part, pl.ds(stream * last, last), :] = summed.astype(z_wire.dtype)
        for distance in Z_FAR_FIRST:
            z_copy(part, distance).start()

    def settled(part, height):
        stream = height // (Z // STREAMS)
        start = core * per_core + stream * stream_rows + (height % (Z // STREAMS)) * z_rows
        start += pick([starts[STEPS] for starts in kept], stream)
        return amps.at[part, rows_at(start, z_rows), :]

    def zg_copy(part, distance, source, to):
        return remote(
            settled(part, source), settled(part, source),
            zg_send.at[part, distance - 1], zg_arrive.at[part, distance - 1], z_device(to),
        )

    def divide(part):
        share = z_total[part, rows_at(z * z_rows, z_rows), :]
        for distance in range(1, Z):
            z_copy(part, distance).wait_recv()
            share = share + z_recv[part, distance - 1].astype(jnp.float32)
        settled(part, z)[...] = (
            share / below[:, part * columns : (part + 1) * columns]
        ).astype(amps.dtype)
        for distance in Z_FAR_FIRST:
            zg_copy(part, distance, z, z_peer(distance)).start()

    def ag_piece(step, slot, arriving):
        part, stream = slot // STREAMS, slot % STREAMS
        size = stream_rows >> (step + 1)
        bit = bits[(stream + step) % STREAMS]
        bit = 1 - bit if arriving else bit
        start = core * per_core + stream * stream_rows + kept[stream][step] + size * bit
        return amps.at[part, rows_at(start, size), :]

    def ag_copy(step, slot, arriving=False):
        piece = ag_piece(step, slot, arriving)
        return remote(
            piece, piece, ag_send.at[step, slot], ag_recv.at[step, slot],
            partner((slot % STREAMS + step) % STREAMS),
        )

    def cross_copy(late, slot, which_core):
        part, stream = slot // STREAMS, slot % STREAMS
        bit = 1 - bits[stream] if late else bits[stream]
        start = which_core * per_core + stream * stream_rows + width * bit
        piece = amps.at[part, rows_at(start, width), :]
        return remote(
            piece, piece, cross_send.at[late, slot], cross_recv.at[late, slot], other_core
        )

    def gather(part, step):
        if step == STEPS - 1:
            for distance in range(1, Z):
                source = z_peer(Z - distance)
                zg_copy(part, distance, source, source).wait_recv()
        for slot in slots_of(part):
            if step < STEPS - 1:
                ag_copy(step + 1, slot, True).wait_recv()
            ag_copy(step, slot).start()
        if step == 0:
            for slot in slots_of(part):
                cross_copy(0, slot, core).start()

    stages = {
        "halve1": lambda part: halve(part, 1),
        "halve2": lambda part: halve(part, 2),
        "halve3": lambda part: halve(part, 3),
        "z": along_z,
        "settle": divide,
        "gather3": lambda part: gather(part, 3),
        "gather2": lambda part: gather(part, 2),
        "gather1": lambda part: gather(part, 1),
        "gather0": lambda part: gather(part, 0),
    }
    wave = [
        (STAGE_TIME[stage] + part * PART_DELAY, order, part, stages[stage])
        for order, stage in enumerate(stages)
        for part in range(PARTS)
    ]
    for pair in range(PARTS // PAIR):
        start = pair * PAIR * PART_DELAY
        wave.append((start, -2, pair, first_sends))
        wave.append((start + STAGE_TIME["keep"], -1, pair, first_keeps))
    for _, _, which, stage in sorted(wave, key=lambda entry: entry[:3]):
        stage(which)

    def terms(position):
        tile = tile_at(position)
        amp = jnp.concatenate(
            [amps[part, rows_at(tile * width, width), :] for part in range(PARTS)], axis=1
        )
        block_p = both[core, table[tile, 0]]
        block_q = both[core, table[tile, 1]]
        to_first = lax.dot_general(
            block_q, amp, (((1,), (1,)), ((), ())), preferred_element_type=jnp.float32
        )
        sums[2 * position + 1] = sums[prev[2 * position]] + to_first
        to_second = jnp.dot(block_p, amp, preferred_element_type=jnp.float32)
        sums[2 * position + 2] = sums[prev[2 * position + 1]] + to_second

    def many_terms(group):
        for stream in range(STREAMS):
            terms(group * STREAMS + stream)

    slots = range(PARTS * STREAMS)
    many_terms(0)
    for slot in slots:
        cross_copy(0, slot, 1 - core).wait_recv()
    many_terms(1)
    for slot in slots:
        ag_copy(0, slot, True).wait_recv()
        cross_copy(1, slot, core).start()
    many_terms(2)
    for slot in slots:
        cross_copy(1, slot, 1 - core).wait_recv()
    many_terms(3)

    def back_copies(distance, source):
        to = orb_peer(distance)
        return [
            remote(
                gamma.at[distance, block], out.at[block, rows_at(source * rows, rows), :],
                back_send.at[distance - 1, block], back_recv.at[distance - 1, block],
                {"orb": to, "aux": aux},
            )
            for block in range(owned)
        ]

    def finish(distance):
        for block in range(owned):
            gamma[distance, block] = sums[final[distance][block]].astype(
                gamma.dtype
            )

    for distance in FAR_FIRST:
        finish(distance)
        for copy in back_copies(distance, orb):
            copy.start()
    finish(0)
    own_out = [
        pltpu.make_async_copy(
            gamma.at[0, block], out.at[block, rows_at(orb * rows, rows), :], local_sem.at[1, block]
        )
        for block in range(owned)
    ]
    for copy in own_out:
        copy.start()

    for distance in range(ORB):
        swap_copy(distance, core).wait_send()
    for distance in range(1, ORB):
        for copy in in_copies(distance, orb):
            copy.wait_send()
    for slot in slots:
        for step in range(STEPS):
            rs_copy(step, slot).wait_send()
            ag_copy(step, slot).wait_send()
        for late in range(2):
            cross_copy(late, slot, core).wait_send()
    for part in range(PARTS):
        for distance in range(1, Z):
            z_copy(part, distance).wait_send()
            zg_copy(part, distance, z, z_peer(distance)).wait_send()
    for distance in range(1, ORB):
        for copy in back_copies(distance, orb):
            copy.wait_send()
        for copy in back_copies(distance, orb_peer(ORB - distance)):
            copy.wait_recv()
    for copy in own_out:
        copy.wait()


def shards(factors, occ_energy, virt_energy, tile_table):
    owned, shard_rows, width = factors.shape
    blocks = owned * ORB
    rows = shard_rows // ORB
    tiles = tile_table.shape[0]
    stream_rows = tiles * width // CORES // STREAMS
    columns = width // PARTS
    slots = PARTS * STREAMS
    halves = [stream_rows >> (step + 1) for step in range(STEPS)]
    last = halves[-1] * STREAMS
    wire = [
        pltpu.VMEM((slots, half, columns), WIRE[step]) for step, half in enumerate(halves)
    ]
    dma = pltpu.SemaphoreType.DMA
    return pl.pallas_call(
        kernel,
        out_shape=jax.ShapeDtypeStruct(factors.shape, factors.dtype),
        in_specs=[
            pl.BlockSpec(memory_space=pltpu.SMEM),
            pl.BlockSpec(memory_space=pltpu.SMEM),
            pl.BlockSpec(memory_space=pl.ANY),
            pl.BlockSpec(memory_space=pltpu.VMEM),
        ],
        out_specs=pl.BlockSpec(memory_space=pl.ANY),
        scratch_shapes=[
            pltpu.VMEM((CORES, blocks, rows, width), jnp.bfloat16),
            *wire,
            *wire,
            pltpu.VMEM((slots, halves[0], columns), jnp.float32),
            pltpu.VMEM((PARTS, last, columns), jnp.float32),
            pltpu.VMEM((PARTS, last, columns), jnp.bfloat16),
            pltpu.VMEM((PARTS, Z - 1, last // Z, columns), jnp.bfloat16),
            pltpu.VMEM((PARTS, tiles * width, columns), jnp.bfloat16),
            pltpu.VMEM((2 * tiles + 1, rows, width), jnp.float32),
            pltpu.VMEM((ORB, owned, rows, width), jnp.bfloat16),
            dma((ORB - 1, owned)),
            dma((ORB - 1, owned)),
            dma((ORB,)),
            dma((ORB,)),
            dma((STEPS, slots)),
            dma((STEPS, slots)),
            dma((PARTS, Z - 1)),
            dma((PARTS, Z - 1)),
            dma((PARTS, Z - 1)),
            dma((PARTS, Z - 1)),
            dma((STEPS, slots)),
            dma((STEPS, slots)),
            dma((2, slots)),
            dma((2, slots)),
            dma((ORB - 1, owned)),
            dma((ORB - 1, owned)),
            dma((2, owned)),
        ],
        compiler_params=pltpu.CompilerParams(
            collective_id=0, has_side_effects=True, vmem_limit_bytes=56 << 20
        ),
        name="window",
    )(tile_table, occ_energy, factors, virt_energy)


def solution(mesh):
    return jax.shard_map(
        shards,
        mesh=mesh,
        in_specs=(P("orb", "aux", None), P(), P(), P()),
        out_specs=P("orb", "aux", None),
        check_vma=False,
    )
```

```python
import jax
import jax.numpy as jnp
from jax import lax
from jax.experimental import pallas as pl
from jax.experimental.pallas import tpu as pltpu
from jax.sharding import PartitionSpec as P

MESH = pl.DeviceIdType.MESH
STREAMS = 4
STEPS = 4
PARTS = 4
PAIR = 2
STAGE_TIME = {
    "keep": 0.5, "halve1": 5.0, "halve2": 8.0, "halve3": 10.5, "z": 12.5, "settle": 19.0,
    "gather3": 24.5, "gather2": 26.5, "gather1": 29.0, "gather0": 32.0,
}
PART_DELAY = 0.3
WIRE = (jnp.bfloat16, jnp.bfloat16, jnp.bfloat16, jnp.float32)
Z = 8
CORES = 2
ORB = 8
FAR_FIRST = (3, 5, 1, 7, 4, 2, 6)
Z_FAR_FIRST = (4, 3, 5, 2, 6, 1, 7)
ARRIVAL = (3, 5, 4, 2, 6, 1, 7)


def device(x, y, z, core):
    return {"orb": y * 2 + z // 4, "aux": x * 8 + (z % 4) * 2 + core}


def pick(options, index):
    if isinstance(index, int):
        return options[index]
    value = options[-1]
    for position in range(len(options) - 2, -1, -1):
        value = jnp.where(index == position, options[position], value)
    return value


def rows_at(start, size):
    return pl.ds(pl.multiple_of(start, size), size)


def kernel(
    table, occ, factors, virt, out,
    both, send_0, send_1, send_2, send_3, recv_0, recv_1, recv_2, recv_3,
    total, z_total, z_wire, z_recv, amps, sums, gamma,
    in_send, in_recv, swap_send, swap_recv, rs_send, rs_recv, z_send, z_arrive,
    zg_send, zg_arrive, ag_send, ag_recv, cross_send, cross_recv, back_send, back_recv, local_sem,
):
    orb = lax.axis_index("orb")
    aux = lax.axis_index("aux")
    x, y, core = aux // 8, orb // 2, aux % 2
    z = (orb % 2) * 4 + (aux // 2) % 4
    near_x, far_x = x + 1 - 2 * (x % 2), 3 - x
    near_y, far_y = y + 1 - 2 * (y % 2), 3 - y
    bits = (((x + 1) // 2) % 2, ((y + 1) // 2) % 2, x // 2, y // 2)
    across_x = (near_x, x, far_x, x)
    across_y = (y, near_y, y, far_y)
    other_core = device(x, y, z, 1 - core)

    sends = (send_0, send_1, send_2, send_3)
    recvs = (recv_0, recv_1, recv_2, recv_3)
    owned, shard_rows, width = factors.shape
    blocks = both.shape[1]
    rows = shard_rows // ORB
    tiles = table.shape[0]
    per_core = amps.shape[1] // CORES
    core_tiles = tiles // CORES
    stream_rows = per_core // STREAMS
    last = stream_rows >> STEPS
    z_rows = last * STREAMS // Z
    columns = width // PARTS
    kept = []
    for stream in range(STREAMS):
        starts = [0]
        for step in range(STEPS):
            starts.append(
                starts[-1] + (stream_rows >> (step + 1)) * bits[(stream + step) % STREAMS]
            )
        kept.append(starts)

    def partner(dim):
        return device(pick(across_x, dim), pick(across_y, dim), z, core)

    def orb_peer(distance):
        return (orb + distance) % ORB

    def z_peer(distance):
        return (z + distance) % Z

    def z_device(height):
        return device(x, y, height, core)

    def remote(src, dst, send_sem, recv_sem, to):
        return pltpu.make_async_remote_copy(
            src_ref=src, dst_ref=dst, send_sem=send_sem, recv_sem=recv_sem,
            device_id=to, device_id_type=MESH,
        )

    barrier = pltpu.get_barrier_semaphore()
    peers = [other_core, partner(0), partner(2)]
    peers += [{"orb": orb_peer(d), "aux": aux} for d in range(1, ORB)]
    peers += [z_device(z_peer(d)) for d in range(1, Z) if d != Z // 2]
    for peer in peers:
        pl.semaphore_signal(barrier, inc=1, device_id=peer, device_id_type=MESH)
    pl.semaphore_wait(barrier, len(peers))

    def slices_of(source, which_core):
        return both.at[which_core, rows_at(source * owned, owned)]

    def in_copies(distance, source):
        to = orb_peer(distance)
        return [
            remote(
                factors.at[block, rows_at(to * rows, rows), :],
                both.at[core, source * owned + block],
                in_send.at[distance - 1, block], in_recv.at[distance - 1, block],
                {"orb": to, "aux": aux},
            )
            for block in range(owned)
        ]

    def swap_copy(distance, which_core):
        source = orb_peer(ORB - distance)
        piece = slices_of(source, which_core)
        return remote(piece, piece, swap_send.at[distance], swap_recv.at[distance], other_core)

    own_in = [
        pltpu.make_async_copy(
            factors.at[block, rows_at(orb * rows, rows), :],
            both.at[core, orb * owned + block],
            local_sem.at[0, block],
        )
        for block in range(owned)
    ]
    for distance in FAR_FIRST:
        for copy in in_copies(distance, orb):
            copy.start()
    for copy in own_in:
        copy.start()

    def tile_at(position):
        group, stream = position // STREAMS, position % STREAMS
        which_core = pick((core, 1 - core, core, 1 - core), group)
        bit = pick(bits, stream)
        bit = pick((bit, bit, 1 - bit, 1 - bit), group)
        return which_core * core_tiles + 2 * stream + bit

    dest = [table[tile_at(term // 2), term % 2] for term in range(2 * tiles)]

    def slot_of(block, before):
        slot = jnp.int32(0)
        for term in range(before):
            slot = jnp.where(dest[term] == block, term + 1, slot)
        return slot

    prev = [slot_of(dest[term], term) for term in range(2 * tiles)]
    final = [
        [slot_of(orb_peer(distance) * owned + block, 2 * tiles) for block in range(owned)]
        for distance in range(ORB)
    ]
    sums[0] = jnp.zeros(sums.shape[1:], sums.dtype)

    settle_stream = z // (Z // STREAMS)
    settle_start = settle_stream * stream_rows + (z % (Z // STREAMS)) * z_rows
    settle_start += pick([starts[STEPS] for starts in kept], settle_stream)
    settle_tile = core * core_tiles + settle_start // width
    first, second = table[settle_tile, 0], table[settle_tile, 1]
    lanes = lax.broadcasted_iota(jnp.int32, (z_rows, width), 1)
    wanted = lax.broadcasted_iota(jnp.int32, (z_rows, width), 0) + settle_start % width
    row_p = jnp.broadcast_to(virt[pl.ds(first, 1), :], (z_rows, width))
    energy_p = jnp.sum(jnp.where(lanes == wanted, row_p, 0.0), axis=1, keepdims=True)
    below = energy_p + virt[pl.ds(second, 1), :] - occ[first] - occ[second]

    for copy in own_in:
        copy.wait()
    swap_copy(0, core).start()
    for distance in ARRIVAL:
        for copy in in_copies(distance, orb_peer(ORB - distance)):
            copy.wait_recv()
        swap_copy(distance, core).start()
    for distance in range(ORB):
        swap_copy(distance, 1 - core).wait_recv()

    def product(tile, pair):
        block_p = both[:, table[core * core_tiles + tile, 0]]
        block_q = both[
            :, table[core * core_tiles + tile, 1], :, pl.ds(pair * PAIR * columns, PAIR * columns)
        ]
        return lax.dot_general(
            block_p.reshape(CORES * rows, width),
            block_q.reshape(CORES * rows, PAIR * columns),
            (((0,), (0,)), ((), ())),
            preferred_element_type=jnp.float32,
        )

    def first_sends(pair):
        def body(stream, carry):
            away = product(2 * stream + 1 - pick(bits, stream), pair).astype(send_0.dtype)
            for member in range(PAIR):
                slot = (pair * PAIR + member) * STREAMS + stream
                send_0[slot] = away[:, member * columns : (member + 1) * columns]
                remote(
                    send_0.at[slot], recv_0.at[slot],
                    rs_send.at[0, slot], rs_recv.at[0, slot], partner(stream),
                ).start()
            return carry

        lax.fori_loop(0, STREAMS, body, 0)

    def first_keeps(pair):
        def body(stream, carry):
            stay = product(2 * stream + pick(bits, stream), pair)
            for member in range(PAIR):
                slot = (pair * PAIR + member) * STREAMS + stream
                total[slot] = stay[:, member * columns : (member + 1) * columns]
            return carry

        lax.fori_loop(0, STREAMS, body, 0)

    def rs_copy(step, slot):
        return remote(
            sends[step].at[slot], recvs[step].at[slot],
            rs_send.at[step, slot], rs_recv.at[step, slot],
            partner((slot % STREAMS + step) % STREAMS),
        )

    def slots_of(part):
        return range(part * STREAMS, (part + 1) * STREAMS)

    def halve(part, step):
        half = stream_rows >> (step + 1)
        for slot in slots_of(part):
            stream = slot % STREAMS
            bit = bits[(stream + step) % STREAMS]
            base = kept[stream][step] - kept[stream][1]
            rs_copy(step - 1, slot).wait_recv()
            sends[step][slot] = (
                total[slot, rows_at(base + half * (1 - bit), half), :]
                + recvs[step - 1][slot, rows_at(half * (1 - bit), half), :]
            ).astype(sends[step].dtype)
            rs_copy(step, slot).start()
        for slot in slots_of(part):
            stream = slot % STREAMS
            bit = bits[(stream + step) % STREAMS]
            base = kept[stream][step] - kept[stream][1]
            total[slot, rows_at(base + half * bit, half), :] += recvs[step - 1][
                slot, rows_at(half * bit, half), :
            ].astype(jnp.float32)

    def z_copy(part, distance):
        to = z_peer(distance)
        return remote(
            z_wire.at[part, rows_at(to * z_rows, z_rows), :],
            z_recv.at[part, distance - 1],
            z_send.at[part, distance - 1], z_arrive.at[part, distance - 1], z_device(to),
        )

    def along_z(part):
        for stream in range(STREAMS):
            slot = part * STREAMS + stream
            rs_copy(STEPS - 1, slot).wait_recv()
            base = kept[stream][STEPS] - kept[stream][1]
            summed = total[slot, rows_at(base, last), :] + recvs[STEPS - 1][slot]
            z_total[part, pl.ds(stream * last, last), :] = summed
            z_wire[part, pl.ds(stream * last, last), :] = summed.astype(z_wire.dtype)
        for distance in Z_FAR_FIRST:
            z_copy(part, distance).start()

    def settled(part, height):
        stream = height // (Z // STREAMS)
        start = core * per_core + stream * stream_rows + (height % (Z // STREAMS)) * z_rows
        start += pick([starts[STEPS] for starts in kept], stream)
        return amps.at[part, rows_at(start, z_rows), :]

    def zg_copy(part, distance, source, to):
        return remote(
            settled(part, source), settled(part, source),
            zg_send.at[part, distance - 1], zg_arrive.at[part, distance - 1], z_device(to),
        )

    def divide(part):
        share = z_total[part, rows_at(z * z_rows, z_rows), :]
        for distance in range(1, Z):
            z_copy(part, distance).wait_recv()
            share = share + z_recv[part, distance - 1].astype(jnp.float32)
        settled(part, z)[...] = (
            share / below[:, part * columns : (part + 1) * columns]
        ).astype(amps.dtype)
        for distance in Z_FAR_FIRST:
            zg_copy(part, distance, z, z_peer(distance)).start()

    def ag_piece(step, slot, arriving):
        part, stream = slot // STREAMS, slot % STREAMS
        size = stream_rows >> (step + 1)
        bit = bits[(stream + step) % STREAMS]
        bit = 1 - bit if arriving else bit
        start = core * per_core + stream * stream_rows + kept[stream][step] + size * bit
        return amps.at[part, rows_at(start, size), :]

    def ag_copy(step, slot, arriving=False):
        piece = ag_piece(step, slot, arriving)
        return remote(
            piece, piece, ag_send.at[step, slot], ag_recv.at[step, slot],
            partner((slot % STREAMS + step) % STREAMS),
        )

    def cross_copy(late, slot, which_core):
        part, stream = slot // STREAMS, slot % STREAMS
        bit = 1 - bits[stream] if late else bits[stream]
        start = which_core * per_core + stream * stream_rows + width * bit
        piece = amps.at[part, rows_at(start, width), :]
        return remote(
            piece, piece, cross_send.at[late, slot], cross_recv.at[late, slot], other_core
        )

    def gather(part, step):
        if step == STEPS - 1:
            for distance in range(1, Z):
                source = z_peer(Z - distance)
                zg_copy(part, distance, source, source).wait_recv()
        for slot in slots_of(part):
            if step < STEPS - 1:
                ag_copy(step + 1, slot, True).wait_recv()
            ag_copy(step, slot).start()
        if step == 0:
            for slot in slots_of(part):
                cross_copy(0, slot, core).start()

    stages = {
        "halve1": lambda part: halve(part, 1),
        "halve2": lambda part: halve(part, 2),
        "halve3": lambda part: halve(part, 3),
        "z": along_z,
        "settle": divide,
        "gather3": lambda part: gather(part, 3),
        "gather2": lambda part: gather(part, 2),
        "gather1": lambda part: gather(part, 1),
        "gather0": lambda part: gather(part, 0),
    }
    wave = [
        (STAGE_TIME[stage] + part * PART_DELAY, order, part, stages[stage])
        for order, stage in enumerate(stages)
        for part in range(PARTS)
    ]
    for pair in range(PARTS // PAIR):
        start = pair * PAIR * PART_DELAY
        wave.append((start, -2, pair, first_sends))
        wave.append((start + STAGE_TIME["keep"], -1, pair, first_keeps))
    for _, _, which, stage in sorted(wave, key=lambda entry: entry[:3]):
        stage(which)

    def terms(position):
        tile = tile_at(position)
        amp = jnp.concatenate(
            [amps[part, rows_at(tile * width, width), :] for part in range(PARTS)], axis=1
        )
        block_p = both[core, table[tile, 0]]
        block_q = both[core, table[tile, 1]]
        to_first = lax.dot_general(
            block_q, amp, (((1,), (1,)), ((), ())), preferred_element_type=jnp.float32
        )
        sums[2 * position + 1] = sums[prev[2 * position]] + to_first
        to_second = jnp.dot(block_p, amp, preferred_element_type=jnp.float32)
        sums[2 * position + 2] = sums[prev[2 * position + 1]] + to_second

    def many_terms(group):
        for stream in range(STREAMS):
            terms(group * STREAMS + stream)

    slots = range(PARTS * STREAMS)
    many_terms(0)
    for slot in slots:
        cross_copy(0, slot, 1 - core).wait_recv()
    many_terms(1)
    for slot in slots:
        ag_copy(0, slot, True).wait_recv()
        cross_copy(1, slot, core).start()
    many_terms(2)
    for slot in slots:
        cross_copy(1, slot, 1 - core).wait_recv()
    many_terms(3)

    def back_copies(distance, source):
        to = orb_peer(distance)
        return [
            remote(
                gamma.at[distance, block], out.at[block, rows_at(source * rows, rows), :],
                back_send.at[distance - 1, block], back_recv.at[distance - 1, block],
                {"orb": to, "aux": aux},
            )
            for block in range(owned)
        ]

    def finish(distance):
        for block in range(owned):
            gamma[distance, block] = sums[final[distance][block]].astype(
                gamma.dtype
            )

    for distance in FAR_FIRST:
        finish(distance)
        for copy in back_copies(distance, orb):
            copy.start()
    finish(0)
    own_out = [
        pltpu.make_async_copy(
            gamma.at[0, block], out.at[block, rows_at(orb * rows, rows), :], local_sem.at[1, block]
        )
        for block in range(owned)
    ]
    for copy in own_out:
        copy.start()

    for distance in range(ORB):
        swap_copy(distance, core).wait_send()
    for distance in range(1, ORB):
        for copy in in_copies(distance, orb):
            copy.wait_send()
    for slot in slots:
        for step in range(STEPS):
            rs_copy(step, slot).wait_send()
            ag_copy(step, slot).wait_send()
        for late in range(2):
            cross_copy(late, slot, core).wait_send()
    for part in range(PARTS):
        for distance in range(1, Z):
            z_copy(part, distance).wait_send()
            zg_copy(part, distance, z, z_peer(distance)).wait_send()
    for distance in range(1, ORB):
        for copy in back_copies(distance, orb):
            copy.wait_send()
        for copy in back_copies(distance, orb_peer(ORB - distance)):
            copy.wait_recv()
    for copy in own_out:
        copy.wait()


def shards(factors, occ_energy, virt_energy, tile_table):
    owned, shard_rows, width = factors.shape
    blocks = owned * ORB
    rows = shard_rows // ORB
    tiles = tile_table.shape[0]
    stream_rows = tiles * width // CORES // STREAMS
    columns = width // PARTS
    slots = PARTS * STREAMS
    halves = [stream_rows >> (step + 1) for step in range(STEPS)]
    last = halves[-1] * STREAMS
    wire = [
        pltpu.VMEM((slots, half, columns), WIRE[step]) for step, half in enumerate(halves)
    ]
    dma = pltpu.SemaphoreType.DMA
    return pl.pallas_call(
        kernel,
        out_shape=jax.ShapeDtypeStruct(factors.shape, factors.dtype),
        in_specs=[
            pl.BlockSpec(memory_space=pltpu.SMEM),
            pl.BlockSpec(memory_space=pltpu.SMEM),
            pl.BlockSpec(memory_space=pl.ANY),
            pl.BlockSpec(memory_space=pltpu.VMEM),
        ],
        out_specs=pl.BlockSpec(memory_space=pl.ANY),
        scratch_shapes=[
            pltpu.VMEM((CORES, blocks, rows, width), jnp.bfloat16),
            *wire,
            *wire,
            pltpu.VMEM((slots, halves[0], columns), jnp.float32),
            pltpu.VMEM((PARTS, last, columns), jnp.float32),
            pltpu.VMEM((PARTS, last, columns), jnp.bfloat16),
            pltpu.VMEM((PARTS, Z - 1, last // Z, columns), jnp.bfloat16),
            pltpu.VMEM((PARTS, tiles * width, columns), jnp.bfloat16),
            pltpu.VMEM((2 * tiles + 1, rows, width), jnp.float32),
            pltpu.VMEM((ORB, owned, rows, width), jnp.bfloat16),
            dma((ORB - 1, owned)),
            dma((ORB - 1, owned)),
            dma((ORB,)),
            dma((ORB,)),
            dma((STEPS, slots)),
            dma((STEPS, slots)),
            dma((PARTS, Z - 1)),
            dma((PARTS, Z - 1)),
            dma((PARTS, Z - 1)),
            dma((PARTS, Z - 1)),
            dma((STEPS, slots)),
            dma((STEPS, slots)),
            dma((2, slots)),
            dma((2, slots)),
            dma((ORB - 1, owned)),
            dma((ORB - 1, owned)),
            dma((2, owned)),
        ],
        compiler_params=pltpu.CompilerParams(
            collective_id=0, has_side_effects=True, vmem_limit_bytes=56 << 20
        ),
        name="window",
    )(tile_table, occ_energy, factors, virt_energy)


def solution(mesh):
    return jax.shard_map(
        shards,
        mesh=mesh,
        in_specs=(P("orb", "aux", None), P(), P(), P()),
        out_specs=P("orb", "aux", None),
        check_vma=False,
    )
```
